32 devices in a mesh: seq: 8 (over z, y), head: 4 (over x, core).
Axes of the slice: x: 2, y: 2, z: 4, core: 2. Of those that a mesh axis runs over, the one named last changes fastest.
Arguments:
- tokens: bfloat16 [2048, 2560], P('seq'), may hold values from -6 to 6
- x_weight: bfloat16 [2560, 5120], P(None, 'head'), may hold values from -0.125 to 0.125
- b_input: bfloat16 [2048, 128], P('seq'), may hold values from -6 to 6
- c_input: bfloat16 [2048, 128], P('seq'), may hold values from -0.52734375 to 0.52734375
- log_decay: float32 [2048, 80], P('seq', 'head'), may hold values from -1 to 0
- step_size: float32 [2048, 80], P('seq', 'head'), may hold values from 0 to 1
- cotangent: bfloat16 [2048, 5120], P('seq', 'head'), may hold values from -6 to 6
Outputs:
- ssd_out: bfloat16 [2048, 5120], P('seq', 'head')
- tokens_grad: bfloat16 [2048, 2560], P('seq', 'head')
- weight_grad: float32 [2560, 5120], P('seq', 'head')
- decay_grad: float32 [2048, 80], P('seq', 'head')
The draws below stay inside these ranges and needn't reach their ends.
All inputs are finite; a program needn't handle non-finite values.
Results may differ from the reference program's by a relative error of at most 0.0061.
Values sent between devices are 32-bit elements; how exact they have to be, the bound alone decides.
A program may use at most 192 MiB of HBM per device.

```python
import jax
import jax.numpy as jnp
from jax import lax

D = 2560
HEAD_TOTAL = 80
HDIM = 64
NSTATE = 128
SPAN = 256
TOK_DEV = 256
TOKEN_POSITIONS = 2048


def head_rates(key):
    base_key = jax.random.fold_in(key, 7)
    key_list = jax.random.split(base_key, 6)
    fast_share = 4
    fast_heads = jax.random.randint(key_list[0], (HEAD_TOTAL,), 0, 8) < fast_share
    fast_base = jax.random.uniform(key_list[1], (HEAD_TOTAL,), jnp.float32, 1.0 / 50.0, 1.0 / 30.0)
    slow_base = jnp.full((HEAD_TOTAL,), 0.5 / TOKEN_POSITIONS, jnp.float32)
    base_rate = jnp.where(fast_heads, fast_base, slow_base)
    block_factor = jnp.exp(jax.random.uniform(key_list[2], (TOKEN_POSITIONS // TOK_DEV, HEAD_TOTAL), jnp.float32, -0.69, 0.69))
    block_factor = jnp.repeat(block_factor, TOK_DEV, axis=0)
    return (base_rate[None, :] * block_factor, key_list)


def draw_log_decay(key, part):
    decay_rates, key_list = head_rates(key)
    coarse_estimate = jax.random.uniform(key_list[3], (TOKEN_POSITIONS, HEAD_TOTAL), jnp.float32, 0.6, 1.4)
    sample_locations = jax.random.randint(key_list[4], (3, HEAD_TOTAL), 0, TOKEN_POSITIONS)
    loss_values = jax.random.uniform(key_list[5], (3, HEAD_TOTAL), jnp.float32, 0.2, 0.4)
    token_positions = lax.broadcasted_iota(jnp.int32, (TOKEN_POSITIONS, HEAD_TOTAL), 0)
    segment_groups = jnp.zeros((TOKEN_POSITIONS, HEAD_TOTAL), jnp.float32)
    for segment_index in range(3):
        segment_groups = segment_groups + jnp.where(token_positions == sample_locations[segment_index][None, :], -jnp.log(1.0 - loss_values[segment_index])[None, :], 0.0)
    return -(decay_rates * coarse_estimate + segment_groups)


def draw_step_size(key, part):
    decay_rates, key_list = head_rates(key)
    spread = jax.random.uniform(jax.random.fold_in(key, 19), (TOKEN_POSITIONS, HEAD_TOTAL), jnp.float32, 0.7, 1.3)
    return jnp.sqrt(2.0 * decay_rates) * spread


def spiked(entries, rng, source, target, shards_of, factor):
    owner, partner = [(jnp.arange(entries.shape[dim]) // (entries.shape[dim] // shards_of)).reshape([-1 if axis == dim else 1 for axis in range(entries.ndim)]) for dim in (source, target)]
    chosen = jax.random.permutation(rng, shards_of)[partner]
    strong = (owner == chosen) | (owner == (partner + shards_of // 2) % shards_of)
    return jnp.where(strong, factor * entries, entries)


def block_levels(rng, dims, shards, smallest, high):
    gain, own = 1.0, jax.random.fold_in(rng, 6)
    for dim, parts in shards:
        steps = jnp.exp(jax.random.uniform(jax.random.fold_in(own, dim), (parts,), jnp.float32, smallest / len(shards), high / len(shards)))
        gain = gain * jnp.repeat(steps, dims[dim] // parts).reshape([-1 if axis == dim else 1 for axis in range(len(dims))])
    return gain


def normal_values(key, dims, scale, most, shards=(), kind=jnp.bfloat16):
    values = jax.random.normal(key, dims, jnp.float32) * scale
    if len(shards) > 0:
        values = block_levels(key, dims, shards, -0.22, 0.18) * values
    return jnp.clip(values, min=-most, max=most).astype(kind)


def gaussian_with(rng, dims, scale, limit, shards, heavy, kind=jnp.bfloat16):
    result = scale * jax.random.normal(rng, dims, jnp.float32)
    if shards:
        result = result * block_levels(rng, dims, shards, -0.22, 0.18)
    return jnp.clip(spiked(result, jax.random.fold_in(rng, 3), *heavy), -limit, limit).astype(kind)


def setup_inputs(seed: int = 0) -> dict:
    keys = jax.random.split(jax.random.key(seed), 8)
    return {
        "tokens": gaussian_with(keys[0], (TOKEN_POSITIONS, D), 1.0, 6.0, ((0, 8),), (0, 1, 8, 2.0)),
        "x_weight": normal_values(keys[1], (D, HEAD_TOTAL * HDIM), D ** -0.5, 0.125, ((1, 4),)),
        "b_input": normal_values(keys[2], (TOKEN_POSITIONS, NSTATE), 1.0, 6.0, ((0, 8),)),
        "c_input": normal_values(keys[3], (TOKEN_POSITIONS, NSTATE), (NSTATE ** -0.5), 0.52734375, ((0, 8),)),
        "log_decay": draw_log_decay(jax.random.fold_in(keys[7], 71), 0),
        "step_size": draw_step_size(jax.random.fold_in(keys[7], 71), 0),
        "cotangent": normal_values(keys[6], (TOKEN_POSITIONS, HEAD_TOTAL * HDIM), 1.0, 6.0, ((0, 8), (1, 4))),
    }


highest = lax.Precision.HIGHEST


def span_tables(length):
    row_ids = lax.broadcasted_iota(jnp.int32, (length, length), 0)
    col_ids = lax.broadcasted_iota(jnp.int32, (length, length), 1)
    return row_ids >= col_ids, row_ids > col_ids


def span_mixing(b_span, c_span, cum_span, lower_mask):
    scores = jnp.dot(c_span, b_span.T, preferred_element_type=jnp.float32)
    cum_heads = cum_span.T
    log_gap = cum_heads[:, :, None] - cum_heads[:, None, :]
    return scores[None] * jnp.exp(jnp.where(lower_mask[None], log_gap, -jnp.inf))


def span_weights(b_span, c_span, cum_span):
    span_end = cum_span[-1]
    b_weighted = (jnp.exp(span_end[None, :] - cum_span)[:, :, None] * b_span.astype(jnp.float32)[:, None, :]).astype(jnp.bfloat16)
    c_weighted = (jnp.exp(cum_span)[:, :, None] * c_span.astype(jnp.float32)[:, None, :]).astype(jnp.bfloat16)
    return b_weighted, c_weighted, jnp.exp(span_end)


def reference(tokens, x_weight, b_input, c_input, log_decay, step_size, cotangent):
    token_count = tokens.shape[0]
    span_count = token_count // SPAN
    pre_act = jnp.dot(tokens, x_weight, preferred_element_type=jnp.float32)
    activated = jax.nn.silu(pre_act)
    x_scaled = (activated.reshape(token_count, HEAD_TOTAL, HDIM) * step_size[:, :, None]).astype(jnp.bfloat16)
    lower_mask, strict_mask = span_tables(SPAN)
    lower_ones = lower_mask.astype(jnp.float32)
    strict_ones = strict_mask.astype(jnp.float32)
    cum_log = jnp.einsum('qr,krh->kqh', lower_ones, log_decay.reshape(span_count, SPAN, HEAD_TOTAL), precision=highest)
    x_spans = x_scaled.reshape(span_count, SPAN, HEAD_TOTAL, HDIM)
    grad_spans = cotangent.reshape(span_count, SPAN, HEAD_TOTAL, HDIM)
    b_spans = b_input.reshape(span_count, SPAN, NSTATE)
    c_spans = c_input.reshape(span_count, SPAN, NSTATE)
    zero_state = jnp.zeros((HEAD_TOTAL, NSTATE, HDIM), jnp.float32)

    def forward_step(carry_state, pieces):
        x_span, b_span, c_span, cum_span = pieces
        b_weighted, c_weighted, span_factor = span_weights(b_span, c_span, cum_span)
        local_state = jnp.einsum('qhn,qhp->hnp', b_weighted.astype(jnp.float32), x_span.astype(jnp.float32))
        return span_factor[:, None, None] * carry_state + local_state, carry_state

    last_state, prior_states = lax.scan(forward_step, zero_state, (x_spans, b_spans, c_spans, cum_log))

    def backward_step(carry_state, pieces):
        grad_span, b_span, c_span, cum_span = pieces
        b_weighted, c_weighted, span_factor = span_weights(b_span, c_span, cum_span)
        gathered = jnp.einsum('qhn,qhp->hnp', c_weighted.astype(jnp.float32), grad_span.astype(jnp.float32))
        return gathered + span_factor[:, None, None] * carry_state, carry_state

    first_adjoint, later_adjoints = lax.scan(backward_step, zero_state, (grad_spans, b_spans, c_spans, cum_log), reverse=True)

    def span_main(pieces):
        x_span, grad_span, b_span, c_span, cum_span, prior_state, adjoint = pieces
        mixing = span_mixing(b_span, c_span, cum_span, lower_mask)
        rounded = mixing.astype(jnp.bfloat16).astype(jnp.float32)
        b_weighted, c_weighted, span_factor = span_weights(b_span, c_span, cum_span)
        x_float = x_span.astype(jnp.float32)
        grad_float = grad_span.astype(jnp.float32)
        inner_part = jnp.einsum('hqr,rhp->qhp', rounded, x_float)
        carried = jnp.einsum('qhn,hnp->qhp', c_weighted.astype(jnp.float32), prior_state, precision=highest)
        output = (inner_part + carried).astype(jnp.bfloat16)
        back_inner = jnp.einsum('hqr,qhp->rhp', rounded, grad_float)
        back_carried = jnp.einsum('rhn,hnp->rhp', b_weighted.astype(jnp.float32), adjoint, precision=highest)
        grad_x = back_inner + back_carried
        products = jnp.einsum('qhp,rhp->hqr', grad_float, x_float)
        pair_terms = jnp.where(strict_mask[None], mixing * products, 0.0)
        shifts = jnp.sum(pair_terms, axis=2) - jnp.sum(pair_terms, axis=1)
        arrival = jnp.sum(grad_float * carried, axis=2)
        departure = jnp.sum(x_float * back_carried, axis=2)
        through = span_factor * jnp.sum(prior_state * adjoint, axis=(1, 2))
        decay_part = jnp.dot(lower_ones.T, shifts.T + arrival, precision=highest)
        decay_part = decay_part + jnp.dot(strict_ones, departure, precision=highest) + through[None, :]
        return output, grad_x, decay_part

    outputs, grad_x, decay_grad = lax.map(span_main, (x_spans, grad_spans, b_spans, c_spans, cum_log, prior_states, later_adjoints))
    sigmoid_pre = jax.nn.sigmoid(pre_act)
    scaled_grad = (grad_x.reshape(token_count, HEAD_TOTAL, HDIM) * step_size[:, :, None]).reshape(token_count, HEAD_TOTAL * HDIM)
    pre_grad = (scaled_grad * sigmoid_pre * (1.0 + pre_act * (1.0 - sigmoid_pre))).astype(jnp.bfloat16)
    weight_grad = lax.dot_general(tokens, pre_grad, (((0,), (0,)), ((), ())), preferred_element_type=jnp.float32)
    tokens_grad = lax.dot_general(pre_grad, x_weight, (((1,), (1,)), ((), ())), preferred_element_type=jnp.float32).astype(jnp.bfloat16)
    ssd_out = outputs.reshape(token_count, HEAD_TOTAL * HDIM)
    return ssd_out, tokens_grad, weight_grad, decay_grad.reshape(token_count, HEAD_TOTAL)
```

```python
import functools

import jax
import jax.numpy as jnp
from jax import lax
from jax.experimental import pallas as pl
from jax.experimental.pallas import tpu as pltpu
from jax.sharding import PartitionSpec as P

SPAN = 256
LANES = 128
MESH = pl.DeviceIdType.MESH
highest = lax.Precision.HIGHEST
f32 = jnp.float32
bf16 = jnp.bfloat16


def dot_f32(a, b, dims=(((1,), (0,)), ((), ()))):
    return lax.dot_general(a, b, dims, preferred_element_type=f32)


def dot_exact(a, b, dims=(((1,), (0,)), ((), ()))):
    return lax.dot_general(a, b, dims, preferred_element_type=f32, precision=highest)


ROWS = (((0,), (0,)), ((), ()))
COLS = (((1,), (1,)), ((), ()))


def split_two(a):
    high = a.astype(bf16)
    return high, (a - high.astype(f32)).astype(bf16)


def span_kernel(n, swap, *refs):
    tok, xw, b_ref, c_ref, ld, st, cot = refs[:7]
    refs = refs[7:]
    if swap:
        tsend, refs = refs[0], refs[1:]
    y_ref, pg_ref, dg_ref = refs[:3]
    refs = refs[3:]
    if swap:
        trecv, refs = refs[0], refs[1:]
    (x_s, pre_s, ce_s, st_s, cum_t, inner_s, back_s, score_s, loc_f, loc_b, out_f, out_b,
     prior, adj, q1_s, q2_s, th_s, send_f, recv_f, send_b, recv_b, tsend_sem, trecv_sem) = refs
    d = lax.axis_index("seq")
    rows, width = cot.shape
    heads = ld.shape[1]
    hdim = width // heads
    pairs = width // LANES
    per = LANES // hdim

    barrier = pltpu.get_barrier_semaphore()
    if swap:
        for o in range(1, n):
            pl.semaphore_signal(barrier, 1, device_id={"seq": lax.rem(d + o, n)}, device_id_type=MESH)
        pl.semaphore_wait(barrier, n - 1)
    else:
        for o in (1, n - 1):
            pl.semaphore_signal(barrier, 1, device_id={"seq": lax.rem(d + o, n)}, device_id_type=MESH)
        pl.semaphore_wait(barrier, 2)

    def tcopy(o):
        to = lax.rem(d + o, n)
        return pltpu.make_async_remote_copy(
            src_ref=tsend.at[to], dst_ref=trecv.at[o], send_sem=tsend_sem.at[o],
            recv_sem=trecv_sem.at[o], device_id={"seq": to}, device_id_type=MESH)

    if swap:
        trecv[0] = tsend[d]
        for o in range(1, n):
            tcopy(o).start()

    row_ids = lax.broadcasted_iota(jnp.int32, (rows, rows), 0)
    col_ids = lax.broadcasted_iota(jnp.int32, (rows, rows), 1)
    lower = row_ids >= col_ids
    lower_ones = lower.astype(f32)
    decay = ld[...]
    cum = dot_exact(lower_ones, decay)
    cum_t[...] = dot_exact(decay, lower_ones, (((0,), (1,)), ((), ())))
    spread = (lax.broadcasted_iota(jnp.int32, (heads, width), 0)
              == lax.broadcasted_iota(jnp.int32, (heads, width), 1) // hdim).astype(f32)
    wide_cum = dot_exact(cum, spread)
    wide_step = dot_exact(st[...], spread)
    for p in range(pairs):
        ce_s[p] = wide_cum[:, p * LANES:(p + 1) * LANES]
        st_s[p] = wide_step[:, p * LANES:(p + 1) * LANES]
    b_val, c_val = b_ref[...], c_ref[...]
    score_s[...] = jnp.where(lower, dot_f32(c_val, b_val, COLS), 0.0)

    step_cols = 2 * LANES
    for k in range(width // step_cols):
        cols = slice(k * step_cols, (k + 1) * step_cols)
        ce = wide_cum[:, cols]
        gw = (cot[:, cols].astype(f32) * jnp.exp(ce)).astype(bf16)
        grad_k = dot_f32(c_val, gw, ROWS)
        pre = dot_f32(tok[...], xw[:, cols])
        act = pre / (1.0 + jnp.exp(-pre))
        xk = (act * wide_step[:, cols]).astype(bf16)
        xwk = (xk.astype(f32) * jnp.exp(ce[rows - 1:rows] - ce)).astype(bf16)
        state_k = dot_f32(b_val, xwk, ROWS)
        for i in range(2):
            half = slice(i * LANES, (i + 1) * LANES)
            pre_s[2 * k + i] = pre[:, half]
            x_s[2 * k + i] = xk[:, half]
            loc_b[2 * k + i] = grad_k[:, half]
            loc_f[2 * k + i] = state_k[:, half]

    @pl.when(d == 0)
    def _():
        prior[...] = jnp.zeros_like(prior)

    @pl.when(d == n - 1)
    def _():
        adj[...] = jnp.zeros_like(adj)

    def fcopy(k):
        return pltpu.make_async_remote_copy(
            src_ref=out_f.at[k], dst_ref=prior.at[k], send_sem=send_f.at[k], recv_sem=recv_f.at[k],
            device_id={"seq": lax.rem(d + 1, n)}, device_id_type=MESH)

    def bcopy(k):
        return pltpu.make_async_remote_copy(
            src_ref=out_b.at[k], dst_ref=adj.at[k], send_sem=send_b.at[k], recv_sem=recv_b.at[k],
            device_id={"seq": lax.rem(d + n - 1, n)}, device_id_type=MESH)

    lane = lax.broadcasted_iota(jnp.int32, (rows, LANES), 1)

    def mix(p):
        ce = ce_s[p]
        xp = x_s[p]
        gp = cot[:, pl.ds(pl.multiple_of(p * LANES, LANES), LANES)]
        inner = back = None
        for i in range(per):
            gap = ce[:, i * hdim:i * hdim + 1] - cum_t[pl.ds(per * p + i, 1), :]
            m = (score_s[...] * jnp.exp(jnp.minimum(gap, 0.0))).astype(bf16)
            inner_i = dot_f32(m, xp)
            back_i = dot_f32(m, gp, ROWS)
            if inner is None:
                inner, back = inner_i, back_i
            else:
                inner = jnp.where(lane < i * hdim, inner, inner_i)
                back = jnp.where(lane < i * hdim, back, back_i)
        inner_s[p] = inner
        back_s[p] = back

    def chain(s, carry):
        kf = s - d

        @pl.when(jnp.logical_and(kf >= 0, kf < pairs))
        def _():
            @pl.when(d > 0)
            def _():
                fcopy(kf).wait_recv()

            @pl.when(d < n - 1)
            def _():
                out_f[kf] = jnp.exp(ce_s[kf, rows - 1:rows, :]) * prior[kf] + loc_f[kf]
                fcopy(kf).start()

        kb = s - (n - 1 - d)

        @pl.when(jnp.logical_and(kb >= 0, kb < pairs))
        def _():
            @pl.when(d < n - 1)
            def _():
                bcopy(kb).wait_recv()

            @pl.when(d > 0)
            def _():
                out_b[kb] = jnp.exp(ce_s[kb, rows - 1:rows, :]) * adj[kb] + loc_b[kb]
                bcopy(kb).start()

        @pl.when(s < pairs)
        def _():
            mix(s)

        return carry

    lax.fori_loop(0, n - 1 + pairs, chain, 0)

    q1_s[...] = jnp.zeros_like(q1_s)
    q2_s[...] = jnp.zeros_like(q2_s)
    th_s[...] = jnp.zeros_like(th_s)

    def finish(p, carry):
        ce = ce_s[p]
        end = ce[rows - 1:rows]
        at = pl.ds(pl.multiple_of(p * LANES, LANES), LANES)
        grad = cot[:, at].astype(f32)
        x = x_s[p].astype(f32)
        pr, ad = prior[p], adj[p]
        hi, lo = split_two(pr)
        y = inner_s[p] + jnp.exp(ce) * (dot_f32(c_val, hi) + dot_f32(c_val, lo))
        y_ref[:, at] = y.astype(bf16)
        hi, lo = split_two(ad)
        bc = jnp.exp(end - ce) * (dot_f32(b_val, hi) + dot_f32(b_val, lo))
        bi = back_s[p]
        pre = pre_s[p]
        sig = 1.0 / (1.0 + jnp.exp(-pre))
        pg = (bi + bc) * st_s[p] * sig * (1.0 + pre * (1.0 - sig))
        pg_ref[:, at] = pg.astype(bf16).astype(f32)
        pick = (lax.broadcasted_iota(jnp.int32, (LANES, heads), 0) // hdim + per * p
                == lax.broadcasted_iota(jnp.int32, (LANES, heads), 1)).astype(f32)
        q1_s[...] += dot_exact(grad * y - x * bi, pick)
        q2_s[...] += dot_exact(x * bc, pick)
        through = jnp.exp(end) * jnp.sum(pr * ad, axis=0, keepdims=True)
        th_s[...] += dot_exact(jnp.broadcast_to(through, (8, LANES)), pick)
        return carry

    lax.fori_loop(0, pairs, finish, 0)
    strict_ones = (row_ids > col_ids).astype(f32)
    dg_ref[...] = (dot_exact(lower_ones, q1_s[...], ROWS) + dot_exact(strict_ones, q2_s[...])
                   + th_s[0:1, :])

    @pl.when(d < n - 1)
    def _():
        def one(k, carry):
            fcopy(k).wait_send()
            return carry
        lax.fori_loop(0, pairs, one, 0)

    @pl.when(d > 0)
    def _():
        def one(k, carry):
            bcopy(k).wait_send()
            return carry
        lax.fori_loop(0, pairs, one, 0)

    if swap:
        for o in range(1, n):
            tcopy(o).wait()


def span_call(n, swap, *args):
    tokens, x_weight, b_input, _, log_decay, _, cotangent = args[:7]
    rows, width = cotangent.shape
    heads, state = log_decay.shape[1], b_input.shape[1]
    pairs = width // LANES
    vm = pl.BlockSpec(memory_space=pltpu.VMEM)
    outs = [jax.ShapeDtypeStruct((rows, width), bf16), jax.ShapeDtypeStruct((rows, width), f32),
            jax.ShapeDtypeStruct((rows, heads), f32)]
    if swap:
        outs.append(jax.ShapeDtypeStruct(args[7].shape, f32))
    wide = pltpu.VMEM((pairs, rows, LANES), f32)
    states = pltpu.VMEM((pairs, state, LANES), f32)
    dma = pltpu.SemaphoreType.DMA
    flops = 2 * rows * tokens.shape[1] * width
    return pl.pallas_call(
        functools.partial(span_kernel, n, swap),
        out_shape=outs,
        in_specs=[vm] * len(args),
        out_specs=[vm] * len(outs),
        scratch_shapes=[
            pltpu.VMEM((pairs, rows, LANES), bf16), wide, wide, wide, pltpu.VMEM((heads, rows), f32),
            wide, wide, pltpu.VMEM((rows, rows), f32), states, states, states, states, states, states,
            pltpu.VMEM((rows, heads), f32), pltpu.VMEM((rows, heads), f32), pltpu.VMEM((8, heads), f32),
            dma((pairs,)), dma((pairs,)), dma((pairs,)), dma((pairs,)), dma((n,)), dma((n,))],
        compiler_params=pltpu.CompilerParams(
            collective_id=0, has_side_effects=True, vmem_limit_bytes=56 << 20),
        cost_estimate=pl.CostEstimate(flops=flops, bytes_accessed=12 << 20, transcendentals=1 << 20),
        name="span",
    )(*args)


def ring_kernel(n, nh, pg, xw, tq, wg_ref, tg_ref, gat, tokall, part, got, send, recv, tok_send,
                tok_recv, g_send, g_recv):
    d, h = lax.axis_index("seq"), lax.axis_index("head")
    rows, width = pg.shape
    quarter = rows // nh
    tcols = tg_ref.shape[1]
    side = lax.rem(d, 2)
    pos = jnp.where(side == 0, d // 2, n - 1 - d // 2)

    def member(p):
        return jnp.where(p < n // 2, 2 * p, 2 * (n - 1 - p) + 1)

    right, left = member(lax.rem(pos + 1, n)), member(lax.rem(pos + n - 1, n))
    barrier = pltpu.get_barrier_semaphore()
    for to in (right, left):
        pl.semaphore_signal(barrier, 1, device_id={"seq": to}, device_id_type=MESH)
    for o in range(1, nh):
        pl.semaphore_signal(barrier, 1, device_id={"head": lax.rem(h + o, nh)}, device_id_type=MESH)
    pl.semaphore_wait(barrier, 1 + nh)

    def hop(j, q, src):
        return pltpu.make_async_remote_copy(
            src_ref=src, dst_ref=gat.at[j, q], send_sem=send.at[j, q], recv_sem=recv.at[j, q],
            device_id={"seq": right if q < nh // 2 else left}, device_id_type=MESH)

    def first(q):
        return hop(0, q, pg.at[pl.ds(q * quarter, quarter), :])

    order = [q for pair in zip(range(nh // 2), range(nh // 2, nh)) for q in pair]
    for q in order:
        first(q).start()

    def tcopy(o):
        return pltpu.make_async_remote_copy(
            src_ref=tq, dst_ref=tokall.at[o], send_sem=tok_send.at[o], recv_sem=tok_recv.at[o],
            device_id={"head": lax.rem(h + o, nh)}, device_id_type=MESH)

    def gcopy(o):
        return pltpu.make_async_remote_copy(
            src_ref=part.at[o], dst_ref=got.at[o], send_sem=g_send.at[o], recv_sem=g_recv.at[o],
            device_id={"head": lax.rem(h + o, nh)}, device_id_type=MESH)

    for o in range(1, nh):
        tcopy(o).start()
    tokall[0] = tq[...]
    pgb = pg[...].astype(bf16)
    for o in list(range(1, nh)) + [0]:
        to = lax.rem(h + o, nh)
        part[o] = dot_f32(pgb, xw[pl.ds(pl.multiple_of(to * tcols, tcols), tcols), :], COLS)
        if o:
            gcopy(o).start()
    for o in range(1, nh):
        tcopy(o).wait()

    def tok_rows(src, quarters):
        off = lax.rem(d - src + n, n)
        return jnp.concatenate(
            [tokall[lax.rem(h - q + nh, nh), off].astype(bf16) for q in quarters], axis=0)

    wg_ref[...] = dot_f32(tok_rows(d, range(nh)), pgb, ROWS)
    halves = (range(nh // 2), range(nh // 2, nh))

    def step(j, carry):
        for q in order:
            hop(j, q, gat.at[j, q]).wait_recv()

            @pl.when(j < n - 2)
            def _():
                hop(j + 1, q, gat.at[j, q]).start()

        sources = (member(lax.rem(pos + n - 1 - j, n)), member(lax.rem(pos + 1 + j, n)))
        total = wg_ref[...]
        for src, quarters in zip(sources, halves):
            block = jnp.concatenate([gat[j, q].astype(bf16) for q in quarters], axis=0)
            total = total + dot_f32(tok_rows(src, quarters), block, ROWS)
        wg_ref[...] = total
        return carry

    lax.fori_loop(0, n - 1, step, 0)
    total = part[0]
    for o in range(1, nh):
        gcopy(o).wait()
        total = total + got[o]
    tg_ref[...] = total.astype(bf16)
    for q in order:
        first(q).wait_send()

    def drain(j, carry):
        for q in order:
            hop(j, q, gat.at[j - 1, q]).wait_send()
        return carry

    lax.fori_loop(1, n - 1, drain, 0)


def ring_call(n, nh, pg, x_weight, tq):
    rows, width = pg.shape
    depth = x_weight.shape[0]
    cols, tcols = tq.shape[2], depth // nh
    vm = pl.BlockSpec(memory_space=pltpu.VMEM)
    dma = pltpu.SemaphoreType.DMA
    return pl.pallas_call(
        functools.partial(ring_kernel, n, nh),
        out_shape=[jax.ShapeDtypeStruct((cols, width), f32), jax.ShapeDtypeStruct((rows, tcols), bf16)],
        in_specs=[vm] * 3,
        out_specs=[vm] * 2,
        scratch_shapes=[
            pltpu.VMEM((n - 1, nh, rows // nh, width), f32), pltpu.VMEM((nh,) + tq.shape, f32),
            pltpu.VMEM((nh, rows, tcols), f32), pltpu.VMEM((nh, rows, tcols), f32),
            dma((n - 1, nh)), dma((n - 1, nh)), dma((nh,)), dma((nh,)), dma((nh,)), dma((nh,))],
        compiler_params=pltpu.CompilerParams(
            collective_id=1, has_side_effects=True, vmem_limit_bytes=56 << 20),
        cost_estimate=pl.CostEstimate(
            flops=4 * rows * depth * width, bytes_accessed=12 << 20, transcendentals=0),
        name="ring",
    )(pg, x_weight, tq)


def per_device(tokens, x_weight, b_input, c_input, log_decay, step_size, cotangent):
    n, nh = lax.axis_size("seq"), lax.axis_size("head")
    rows, depth = tokens.shape
    assert rows == SPAN and n % 2 == 0
    swap = 4 <= n <= 16
    args = (tokens, x_weight, b_input, c_input, log_decay, step_size, cotangent)
    if swap:
        quarter = rows // nh
        mine = lax.dynamic_slice_in_dim(tokens, lax.axis_index("head") * quarter, quarter, 0)
        mine = jnp.transpose(mine.reshape(quarter, n, depth // n), (1, 0, 2)).astype(f32)
        y, pg, dg, tq = span_call(n, True, *args, mine)
        wg, tg = ring_call(n, nh, pg, x_weight, tq)
        return y, tg, wg, dg
    y, pg, dg = span_call(n, False, *args)
    pgb = pg.astype(bf16)
    wg = lax.psum_scatter(dot_f32(tokens, pgb, ROWS), "seq", scatter_dimension=0, tiled=True)
    tg = lax.psum_scatter(dot_f32(pgb, x_weight, COLS), "head", scatter_dimension=1, tiled=True)
    return y, tg.astype(bf16), wg, dg


def solution(mesh):
    return jax.shard_map(
        per_device,
        mesh=mesh,
        in_specs=(
            P("seq", None),
            P(None, "head"),
            P("seq", None),
            P("seq", None),
            P("seq", "head"),
            P("seq", "head"),
            P("seq", "head"),
        ),
        out_specs=(P("seq", "head"), P("seq", "head"), P("seq", "head"), P("seq", "head")),
        check_vma=False,
    )
```

```python
import functools

import jax
import jax.numpy as jnp
from jax import lax
from jax.experimental import pallas as pl
from jax.experimental.pallas import tpu as pltpu
from jax.sharding import PartitionSpec as P

SPAN = 256
LANES = 128
MESH = pl.DeviceIdType.MESH
highest = lax.Precision.HIGHEST
f32 = jnp.float32
bf16 = jnp.bfloat16


def dot_f32(a, b, dims=(((1,), (0,)), ((), ()))):
    return lax.dot_general(a, b, dims, preferred_element_type=f32)


def dot_exact(a, b, dims=(((1,), (0,)), ((), ()))):
    return lax.dot_general(a, b, dims, preferred_element_type=f32, precision=highest)


ROWS = (((0,), (0,)), ((), ()))
COLS = (((1,), (1,)), ((), ()))


def split_two(a):
    high = a.astype(bf16)
    return high, (a - high.astype(f32)).astype(bf16)


def span_kernel(n, nh, ring, *refs):
    tok, xw, b_ref, c_ref, ld, st, cot = refs[:7]
    refs = refs[7:]
    if ring:
        tsend, y_ref, dg_ref, wg_ref, tg_ref = refs[:5]
        refs = refs[5:]
    else:
        y_ref, pg_ref, dg_ref = refs[:3]
        refs = refs[3:]
    (x_s, pre_s, ce_s, st_s, cum_t, inner_s, back_s, score_s, loc_f, loc_b, out_f, out_b,
     prior, adj, q1_s, q2_s, th_s, send_f, recv_f, send_b, recv_b) = refs[:21]
    if ring:
        (pg_s, gat, tokall, tokmat, part, got, r_send, r_recv, t_send, t_recv, h_send, h_recv,
         g_send, g_recv) = refs[21:]
    d, h = lax.axis_index("seq"), lax.axis_index("head")
    rows, width = cot.shape
    heads = ld.shape[1]
    hdim = width // heads
    pairs = width // LANES
    per = LANES // hdim
    quarter, half = rows // nh, rows // 2

    barrier = pltpu.get_barrier_semaphore()
    for o in range(1, n) if ring else (1, n - 1):
        pl.semaphore_signal(barrier, 1, device_id={"seq": lax.rem(d + o, n)}, device_id_type=MESH)
    if ring:
        for o in range(1, nh):
            pl.semaphore_signal(barrier, 1, device_id={"head": lax.rem(h + o, nh)}, device_id_type=MESH)
    pl.semaphore_wait(barrier, n + nh - 2 if ring else 2)

    if ring:
        side = lax.rem(d, 2)
        pos = jnp.where(side == 0, d // 2, n - 1 - d // 2)

        def member(p):
            return jnp.where(p < n // 2, 2 * p, 2 * (n - 1 - p) + 1)

        next_to = (member(lax.rem(pos + 1, n)), member(lax.rem(pos + n - 1, n)))

        def tcopy(o):
            to = lax.rem(d + o, n)
            return pltpu.make_async_remote_copy(
                src_ref=tsend.at[to], dst_ref=tokall.at[0, o], send_sem=t_send.at[o],
                recv_sem=t_recv.at[o], device_id={"seq": to}, device_id_type=MESH)

        def hcopy(o):
            return pltpu.make_async_remote_copy(
                src_ref=tokall.at[0], dst_ref=tokall.at[o], send_sem=h_send.at[o],
                recv_sem=h_recv.at[o], device_id={"head": lax.rem(h + o, nh)}, device_id_type=MESH)

        def gcopy(o):
            return pltpu.make_async_remote_copy(
                src_ref=part.at[o], dst_ref=got.at[o], send_sem=g_send.at[o], recv_sem=g_recv.at[o],
                device_id={"head": lax.rem(h + o, nh)}, device_id_type=MESH)

        def hop(j, k, w, src):
            return pltpu.make_async_remote_copy(
                src_ref=src, dst_ref=gat.at[j, k, w], send_sem=r_send.at[j, k, w],
                recv_sem=r_recv.at[j, k, w], device_id={"seq": next_to[w]}, device_id_type=MESH)

        tokall[0, 0] = tsend[d]
        for o in range(1, n):
            tcopy(o).start()

    row_ids = lax.broadcasted_iota(jnp.int32, (rows, rows), 0)
    col_ids = lax.broadcasted_iota(jnp.int32, (rows, rows), 1)
    lower = row_ids >= col_ids
    lower_ones = lower.astype(f32)
    decay = ld[...]
    cum = dot_exact(lower_ones, decay)
    cum_t[...] = dot_exact(decay, lower_ones, (((0,), (1,)), ((), ())))
    spread = (lax.broadcasted_iota(jnp.int32, (heads, width), 0)
              == lax.broadcasted_iota(jnp.int32, (heads, width), 1) // hdim).astype(f32)
    wide_cum = dot_exact(cum, spread)
    wide_step = dot_exact(st[...], spread)
    for p in range(pairs):
        ce_s[p] = wide_cum[:, p * LANES:(p + 1) * LANES]
        st_s[p] = wide_step[:, p * LANES:(p + 1) * LANES]
    b_val, c_val = b_ref[...], c_ref[...]
    score_s[...] = jnp.where(lower, dot_f32(c_val, b_val, COLS), 0.0)
    q1_s[...] = jnp.zeros_like(q1_s)
    q2_s[...] = jnp.zeros_like(q2_s)
    th_s[...] = jnp.zeros_like(th_s)

    step_cols = 2 * LANES
    for k in range(width // step_cols):
        cols = slice(k * step_cols, (k + 1) * step_cols)
        ce = wide_cum[:, cols]
        gw = (cot[:, cols].astype(f32) * jnp.exp(ce)).astype(bf16)
        grad_k = dot_f32(c_val, gw, ROWS)
        pre = dot_f32(tok[...], xw[:, cols])
        act = pre / (1.0 + jnp.exp(-pre))
        xk = (act * wide_step[:, cols]).astype(bf16)
        xwk = (xk.astype(f32) * jnp.exp(ce[rows - 1:rows] - ce)).astype(bf16)
        state_k = dot_f32(b_val, xwk, ROWS)
        for i in range(2):
            at = slice(i * LANES, (i + 1) * LANES)
            pre_s[2 * k + i] = pre[:, at]
            x_s[2 * k + i] = xk[:, at]
            loc_b[2 * k + i] = grad_k[:, at]
            loc_f[2 * k + i] = state_k[:, at]

    @pl.when(d == 0)
    def _():
        prior[...] = jnp.zeros_like(prior)

    @pl.when(d == n - 1)
    def _():
        adj[...] = jnp.zeros_like(adj)

    def fcopy(k):
        return pltpu.make_async_remote_copy(
            src_ref=out_f.at[k], dst_ref=prior.at[k], send_sem=send_f.at[k], recv_sem=recv_f.at[k],
            device_id={"seq": lax.rem(d + 1, n)}, device_id_type=MESH)

    def bcopy(k):
        return pltpu.make_async_remote_copy(
            src_ref=out_b.at[k], dst_ref=adj.at[k], send_sem=send_b.at[k], recv_sem=recv_b.at[k],
            device_id={"seq": lax.rem(d + n - 1, n)}, device_id_type=MESH)

    lane = lax.broadcasted_iota(jnp.int32, (rows, LANES), 1)

    def mix(p):
        ce = ce_s[p]
        xp = x_s[p]
        gp = cot[:, pl.ds(pl.multiple_of(p * LANES, LANES), LANES)]
        inner = back = None
        for i in range(per):
            gap = ce[:, i * hdim:i * hdim + 1] - cum_t[pl.ds(per * p + i, 1), :]
            m = (score_s[...] * jnp.exp(jnp.minimum(gap, 0.0))).astype(bf16)
            inner_i = dot_f32(m, xp)
            back_i = dot_f32(m, gp, ROWS)
            if inner is None:
                inner, back = inner_i, back_i
            else:
                inner = jnp.where(lane < i * hdim, inner, inner_i)
                back = jnp.where(lane < i * hdim, back, back_i)
        inner_s[p] = inner
        back_s[p] = back

    def finish(p):
        ce = ce_s[p]
        end = ce[rows - 1:rows]
        at = pl.ds(pl.multiple_of(p * LANES, LANES), LANES)
        pr, ad = prior[p], adj[p]
        hi, lo = split_two(ad)
        bc = jnp.exp(end - ce) * (dot_f32(b_val, hi) + dot_f32(b_val, lo))
        bi = back_s[p]
        pre = pre_s[p]
        sig = 1.0 / (1.0 + jnp.exp(-pre))
        pg = (bi + bc) * st_s[p] * sig * (1.0 + pre * (1.0 - sig))
        pg = pg.astype(bf16).astype(f32)
        if ring:
            pg_s[p, 0] = pg[:half]
            pg_s[p, 1] = pg[half:]
            for w in range(2):
                hop(0, p, w, pg_s.at[p, w]).start()
        else:
            pg_ref[:, at] = pg
        grad = cot[:, at].astype(f32)
        x = x_s[p].astype(f32)
        hi, lo = split_two(pr)
        y = inner_s[p] + jnp.exp(ce) * (dot_f32(c_val, hi) + dot_f32(c_val, lo))
        y_ref[:, at] = y.astype(bf16)
        pick = (lax.broadcasted_iota(jnp.int32, (LANES, heads), 0) // hdim + per * p
                == lax.broadcasted_iota(jnp.int32, (LANES, heads), 1)).astype(f32)
        q1_s[...] += dot_exact(grad * y - x * bi, pick)
        q2_s[...] += dot_exact(x * bc, pick)
        through = jnp.exp(end) * jnp.sum(pr * ad, axis=0, keepdims=True)
        th_s[...] += dot_exact(jnp.broadcast_to(through, (8, LANES)), pick)

    def forward(s):
        def one(k, carry):
            j = s - n - k

            @pl.when(jnp.logical_and(j >= 0, j < n - 1))
            def _():
                for w in range(2):
                    hop(j, k, w, gat.at[j, k, w]).wait_recv()

                    @pl.when(j < n - 2)
                    def _():
                        hop(j + 1, k, w, gat.at[j, k, w]).start()

            return carry

        lax.fori_loop(0, pairs, one, 0)

    def arrange():
        for o in range(1, nh):
            hcopy(o).wait()

        def place(slot, src, q):
            tokmat[slot, q * quarter:(q + 1) * quarter, :] = tokall[
                lax.rem(h - q + nh, nh), lax.rem(d - src + n, n)].astype(bf16)

        def one(slot, carry):
            for q in range(nh):
                p = pos + n - slot if q < nh // 2 else pos + slot
                place(slot, member(lax.rem(p, n)), q)
            return carry

        lax.fori_loop(0, n, one, 0)

    def weights(k):
        blocks = [jnp.concatenate([pg_s[k + i, w] for i in range(2)], axis=1).astype(bf16)
                  for w in range(2)]
        for j in range(n - 1):
            for w in range(2):
                blocks.append(jnp.concatenate(
                    [gat[j, k + i, w] for i in range(2)], axis=1).astype(bf16))
        wg_ref[:, pl.ds(pl.multiple_of(k * LANES, 2 * LANES), 2 * LANES)] = dot_f32(
            tokmat[...].reshape(n * rows, tokmat.shape[2]), jnp.concatenate(blocks, axis=0), ROWS)

    def input_part(o):
        tcols = part.shape[2]
        to = lax.rem(h + o, nh)
        pgb = jnp.concatenate(
            [jnp.concatenate([pg_s[p, w].astype(bf16) for p in range(pairs)], axis=1)
             for w in range(2)], axis=0)
        part[o] = dot_f32(pgb, xw[pl.ds(pl.multiple_of(to * tcols, tcols), tcols), :], COLS)
        if o:
            gcopy(o).start()

    def chain(s, carry):
        if ring:
            forward(s)
        kf = s - d

        @pl.when(jnp.logical_and(kf >= 0, kf < pairs))
        def _():
            @pl.when(d > 0)
            def _():
                fcopy(kf).wait_recv()

            @pl.when(d < n - 1)
            def _():
                out_f[kf] = jnp.exp(ce_s[kf, rows - 1:rows, :]) * prior[kf] + loc_f[kf]
                fcopy(kf).start()

        kb = s - (n - 1 - d)

        @pl.when(jnp.logical_and(kb >= 0, kb < pairs))
        def _():
            @pl.when(d < n - 1)
            def _():
                bcopy(kb).wait_recv()

            @pl.when(d > 0)
            def _():
                out_b[kb] = jnp.exp(ce_s[kb, rows - 1:rows, :]) * adj[kb] + loc_b[kb]
                bcopy(kb).start()

        @pl.when(s < pairs)
        def _():
            mix(s)

        ks = s - (n - 1)

        @pl.when(jnp.logical_and(ks >= 0, ks < pairs))
        def _():
            finish(ks)

        if ring:
            @pl.when(s == n - 2)
            def _():
                for o in range(1, n):
                    tcopy(o).wait()
                for o in range(1, nh):
                    hcopy(o).start()

            for o in range(nh):
                @pl.when(s == n - 1 + pairs + (o - 1) % nh)
                def _():
                    input_part(o)

            @pl.when(s == max(2 * n - 2, n + pairs + nh))
            def _():
                arrange()
        return carry

    total_steps = n - 1 + pairs + (n - 1 if ring else 0)
    lax.fori_loop(0, total_steps, chain, 0)

    strict_ones = (row_ids > col_ids).astype(f32)
    dg_ref[...] = (dot_exact(lower_ones, q1_s[...], ROWS) + dot_exact(strict_ones, q2_s[...])
                   + th_s[0:1, :])

    @pl.when(d < n - 1)
    def _():
        def one(k, carry):
            fcopy(k).wait_send()
            return carry
        lax.fori_loop(0, pairs, one, 0)

    @pl.when(d > 0)
    def _():
        def one(k, carry):
            bcopy(k).wait_send()
            return carry
        lax.fori_loop(0, pairs, one, 0)

    if ring:
        def each(k, carry):
            weights(2 * k)
            return carry

        lax.fori_loop(0, pairs // 2, each, 0)
        total = part[0]
        for o in range(1, nh):
            gcopy(o).wait()
            total = total + got[o]
        tg_ref[...] = total.astype(bf16)

        def drain(k, carry):
            for w in range(2):
                hop(0, k, w, pg_s.at[k, w]).wait_send()

                def one(j, carry):
                    hop(j, k, w, gat.at[j - 1, k, w]).wait_send()
                    return carry

                lax.fori_loop(1, n - 1, one, 0)
            return carry

        lax.fori_loop(0, pairs, drain, 0)


def span_call(n, nh, ring, *args):
    tokens, x_weight, b_input, _, log_decay, _, cotangent = args[:7]
    rows, width = cotangent.shape
    depth = tokens.shape[1]
    heads, state = log_decay.shape[1], b_input.shape[1]
    pairs = width // LANES
    vm = pl.BlockSpec(memory_space=pltpu.VMEM)
    wide = pltpu.VMEM((pairs, rows, LANES), f32)
    states = pltpu.VMEM((pairs, state, LANES), f32)
    dma = pltpu.SemaphoreType.DMA
    scratch = [
        pltpu.VMEM((pairs, rows, LANES), bf16), wide, wide, wide, pltpu.VMEM((heads, rows), f32),
        wide, wide, pltpu.VMEM((rows, rows), f32), states, states, states, states, states, states,
        pltpu.VMEM((rows, heads), f32), pltpu.VMEM((rows, heads), f32), pltpu.VMEM((8, heads), f32),
        dma((pairs,)), dma((pairs,)), dma((pairs,)), dma((pairs,))]
    y = jax.ShapeDtypeStruct((rows, width), bf16)
    dg = jax.ShapeDtypeStruct((rows, heads), f32)
    if ring:
        cols, tcols = depth // n, depth // nh
        outs = [y, dg, jax.ShapeDtypeStruct((cols, width), f32), jax.ShapeDtypeStruct((rows, tcols), bf16)]
        out_part = pltpu.VMEM((nh, rows, tcols), f32)
        scratch += [
            pltpu.VMEM((pairs, 2, rows // 2, LANES), f32),
            pltpu.VMEM((n - 1, pairs, 2, rows // 2, LANES), f32),
            pltpu.VMEM((nh,) + args[7].shape, f32), pltpu.VMEM((n, rows, cols), bf16), out_part, out_part,
            dma((n - 1, pairs, 2)), dma((n - 1, pairs, 2)), dma((n,)), dma((n,)),
            dma((nh,)), dma((nh,)), dma((nh,)), dma((nh,))]
    else:
        outs = [y, jax.ShapeDtypeStruct((rows, width), f32), dg]
    return pl.pallas_call(
        functools.partial(span_kernel, n, nh, ring),
        out_shape=outs,
        in_specs=[vm] * len(args),
        out_specs=[vm] * len(outs),
        scratch_shapes=scratch,
        compiler_params=pltpu.CompilerParams(
            collective_id=0, has_side_effects=True, vmem_limit_bytes=60 << 20),
        cost_estimate=pl.CostEstimate(
            flops=6 * rows * depth * width, bytes_accessed=12 << 20, transcendentals=1 << 20),
        name="span",
    )(*args)


def per_device(tokens, x_weight, b_input, c_input, log_decay, step_size, cotangent):
    n, nh = lax.axis_size("seq"), lax.axis_size("head")
    rows, depth = tokens.shape
    assert rows == SPAN and n % 2 == 0
    ring = 4 <= n <= 8
    args = (tokens, x_weight, b_input, c_input, log_decay, step_size, cotangent)
    if ring:
        quarter = rows // nh
        mine = lax.dynamic_slice_in_dim(tokens, lax.axis_index("head") * quarter, quarter, 0)
        mine = jnp.transpose(mine.reshape(quarter, n, depth // n), (1, 0, 2)).astype(f32)
        y, dg, wg, tg = span_call(n, nh, True, *args, mine)
        return y, tg, wg, dg
    y, pg, dg = span_call(n, nh, False, *args)
    pgb = pg.astype(bf16)
    wg = lax.psum_scatter(dot_f32(tokens, pgb, ROWS), "seq", scatter_dimension=0, tiled=True)
    tg = lax.psum_scatter(dot_f32(pgb, x_weight, COLS), "head", scatter_dimension=1, tiled=True)
    return y, tg.astype(bf16), wg, dg


def solution(mesh):
    return jax.shard_map(
        per_device,
        mesh=mesh,
        in_specs=(
            P("seq", None),
            P(None, "head"),
            P("seq", None),
            P("seq", None),
            P("seq", "head"),
            P("seq", "head"),
            P("seq", "head"),
        ),
        out_specs=(P("seq", "head"), P("seq", "head"), P("seq", "head"), P("seq", "head")),
        check_vma=False,
    )
```

```python
import functools

import jax
import jax.numpy as jnp
from jax import lax
from jax.experimental import pallas as pl
from jax.experimental.pallas import tpu as pltpu
from jax.sharding import PartitionSpec as P

SPAN = 256
LANES = 128
MESH = pl.DeviceIdType.MESH
highest = lax.Precision.HIGHEST
f32 = jnp.float32
bf16 = jnp.bfloat16


def dot_f32(a, b, dims=(((1,), (0,)), ((), ()))):
    return lax.dot_general(a, b, dims, preferred_element_type=f32)


def dot_exact(a, b, dims=(((1,), (0,)), ((), ()))):
    return lax.dot_general(a, b, dims, preferred_element_type=f32, precision=highest)


ROWS = (((0,), (0,)), ((), ()))
COLS = (((1,), (1,)), ((), ()))


def split_two(a):
    high = a.astype(bf16)
    return high, (a - high.astype(f32)).astype(bf16)


def span_kernel(n, nh, ring, *refs):
    tok, xw_hbm, b_ref, c_ref, ld, st, cot = refs[:7]
    refs = refs[7:]
    if ring:
        y_ref, dg_ref, wg_ref, tg_ref = refs[:4]
        refs = refs[4:]
    else:
        y_ref, pg_ref, dg_ref = refs[:3]
        refs = refs[3:]
    (x_s, pre_s, ce_s, st_s, cum_t, inner_s, back_s, score_s, loc_f, loc_b, out_f, out_b,
     prior, adj, q1_s, q2_s, th_s, xw, xw_sem, send_f, recv_f, send_b, recv_b) = refs[:23]
    if ring:
        (pg_s, pg_t, gat, tsend, tokall, tokmat, part, got, r_send, r_recv, t_send, t_recv, h_send, h_recv,
         g_send, g_recv) = refs[23:]
    d, h = lax.axis_index("seq"), lax.axis_index("head")
    rows, width = cot.shape
    heads = ld.shape[0]
    hdim = width // heads
    pairs = width // LANES
    per = LANES // hdim
    quarter, half = rows // nh, rows // 2
    load = pltpu.make_async_copy(xw_hbm, xw, xw_sem)
    load.start()

    barrier = pltpu.get_barrier_semaphore()
    for o in range(1, n) if ring else (1, n - 1):
        pl.semaphore_signal(barrier, 1, device_id={"seq": lax.rem(d + o, n)}, device_id_type=MESH)
    if ring:
        for o in range(1, nh):
            pl.semaphore_signal(barrier, 1, device_id={"head": lax.rem(h + o, nh)}, device_id_type=MESH)
    pl.semaphore_wait(barrier, n + nh - 2 if ring else 2)

    if ring:
        side = lax.rem(d, 2)
        pos = jnp.where(side == 0, d // 2, n - 1 - d // 2)

        def member(p):
            return jnp.where(p < n // 2, 2 * p, 2 * (n - 1 - p) + 1)

        next_to = (member(lax.rem(pos + 1, n)), member(lax.rem(pos + n - 1, n)))

        def tcopy(o):
            to = lax.rem(d + o, n)
            return pltpu.make_async_remote_copy(
                src_ref=tsend.at[to], dst_ref=tokall.at[0, o], send_sem=t_send.at[o],
                recv_sem=t_recv.at[o], device_id={"seq": to}, device_id_type=MESH)

        def hcopy(o):
            return pltpu.make_async_remote_copy(
                src_ref=tokall.at[0], dst_ref=tokall.at[o], send_sem=h_send.at[o],
                recv_sem=h_recv.at[o], device_id={"head": lax.rem(h + o, nh)}, device_id_type=MESH)

        def gcopy(o):
            return pltpu.make_async_remote_copy(
                src_ref=part.at[o], dst_ref=got.at[o], send_sem=g_send.at[o], recv_sem=g_recv.at[o],
                device_id={"head": lax.rem(h + o, nh)}, device_id_type=MESH)

        def hop(j, k, w, src):
            return pltpu.make_async_remote_copy(
                src_ref=src, dst_ref=gat.at[j, k, w], send_sem=r_send.at[j, k, w],
                recv_sem=r_recv.at[j, k, w], device_id={"seq": next_to[w]}, device_id_type=MESH)

        mine = tok[pl.ds(pl.multiple_of(h * quarter, quarter), quarter), :]
        tcols = tsend.shape[2]
        for i in range(n):
            tsend[i] = mine[:, i * tcols:(i + 1) * tcols].astype(f32)
        tokall[0, 0] = tsend[d]
        for o in range(1, n):
            tcopy(o).start()

    row_ids = lax.broadcasted_iota(jnp.int32, (rows, rows), 0)
    col_ids = lax.broadcasted_iota(jnp.int32, (rows, rows), 1)
    lower = row_ids >= col_ids
    lower_ones = lower.astype(f32)
    decay = ld[...]
    cum = dot_exact(lower_ones, decay, COLS)
    cum_t[...] = dot_exact(decay, lower_ones, COLS)
    spread = (lax.broadcasted_iota(jnp.int32, (heads, width), 0)
              == lax.broadcasted_iota(jnp.int32, (heads, width), 1) // hdim).astype(f32)
    wide_cum = dot_exact(cum, spread)
    wide_step = dot_exact(st[...], spread, ROWS)
    for p in range(pairs):
        ce_s[p] = wide_cum[:, p * LANES:(p + 1) * LANES]
        st_s[p] = wide_step[:, p * LANES:(p + 1) * LANES]
    b_val, c_val = b_ref[...], c_ref[...]
    score_s[...] = jnp.where(lower, dot_f32(c_val, b_val, COLS), 0.0)
    q1_s[...] = jnp.zeros_like(q1_s)
    q2_s[...] = jnp.zeros_like(q2_s)
    th_s[...] = jnp.zeros_like(th_s)

    load.wait()
    step_cols = 2 * LANES
    for k in range(width // step_cols):
        cols = slice(k * step_cols, (k + 1) * step_cols)
        ce = wide_cum[:, cols]
        gw = (cot[:, cols].astype(f32) * jnp.exp(ce)).astype(bf16)
        grad_k = dot_f32(c_val, gw, ROWS)
        pre = dot_f32(tok[...], xw[:, cols])
        act = pre / (1.0 + jnp.exp(-pre))
        xk = (act * wide_step[:, cols]).astype(bf16)
        xwk = (xk.astype(f32) * jnp.exp(ce[rows - 1:rows] - ce)).astype(bf16)
        state_k = dot_f32(b_val, xwk, ROWS)
        for i in range(2):
            at = slice(i * LANES, (i + 1) * LANES)
            pre_s[2 * k + i] = pre[:, at]
            x_s[2 * k + i] = xk[:, at]
            loc_b[2 * k + i] = grad_k[:, at]
            loc_f[2 * k + i] = state_k[:, at]

    @pl.when(d == 0)
    def _():
        prior[...] = jnp.zeros_like(prior)

    @pl.when(d == n - 1)
    def _():
        adj[...] = jnp.zeros_like(adj)

    def fcopy(k):
        return pltpu.make_async_remote_copy(
            src_ref=out_f.at[k], dst_ref=prior.at[k], send_sem=send_f.at[k], recv_sem=recv_f.at[k],
            device_id={"seq": lax.rem(d + 1, n)}, device_id_type=MESH)

    def bcopy(k):
        return pltpu.make_async_remote_copy(
            src_ref=out_b.at[k], dst_ref=adj.at[k], send_sem=send_b.at[k], recv_sem=recv_b.at[k],
            device_id={"seq": lax.rem(d + n - 1, n)}, device_id_type=MESH)

    lane = lax.broadcasted_iota(jnp.int32, (rows, LANES), 1)

    def mix(p):
        ce = ce_s[p]
        xp = x_s[p]
        gp = cot[:, pl.ds(pl.multiple_of(p * LANES, LANES), LANES)]
        inner = back = None
        for i in range(per):
            gap = ce[:, i * hdim:i * hdim + 1] - cum_t[pl.ds(per * p + i, 1), :]
            m = (score_s[...] * jnp.exp(jnp.minimum(gap, 0.0))).astype(bf16)
            inner_i = dot_f32(m, xp)
            back_i = dot_f32(m, gp, ROWS)
            if inner is None:
                inner, back = inner_i, back_i
            else:
                inner = jnp.where(lane < i * hdim, inner, inner_i)
                back = jnp.where(lane < i * hdim, back, back_i)
        inner_s[p] = inner
        back_s[p] = back

    def finish(p):
        ce = ce_s[p]
        end = ce[rows - 1:rows]
        at = pl.ds(pl.multiple_of(p * LANES, LANES), LANES)
        pr, ad = prior[p], adj[p]
        hi, lo = split_two(ad)
        bc = jnp.exp(end - ce) * (dot_f32(b_val, hi) + dot_f32(b_val, lo))
        bi = back_s[p]
        pre = pre_s[p]
        sig = 1.0 / (1.0 + jnp.exp(-pre))
        pg = (bi + bc) * st_s[p] * sig * (1.0 + pre * (1.0 - sig))
        pg = pg.astype(bf16).astype(f32)
        if ring:
            pg_t[at, :] = jnp.transpose(pg).astype(bf16)
            pg_s[p, 0] = pg[:half]
            pg_s[p, 1] = pg[half:]
            for w in range(2):
                hop(0, p, w, pg_s.at[p, w]).start()
        else:
            pg_ref[:, at] = pg
        grad = cot[:, at].astype(f32)
        x = x_s[p].astype(f32)
        hi, lo = split_two(pr)
        y = inner_s[p] + jnp.exp(ce) * (dot_f32(c_val, hi) + dot_f32(c_val, lo))
        y_ref[:, at] = y.astype(bf16)
        pick = (lax.broadcasted_iota(jnp.int32, (LANES, heads), 0) // hdim + per * p
                == lax.broadcasted_iota(jnp.int32, (LANES, heads), 1)).astype(f32)
        q1_s[...] += dot_exact(grad * y - x * bi, pick)
        q2_s[...] += dot_exact(x * bc, pick)
        through = jnp.exp(end) * jnp.sum(pr * ad, axis=0, keepdims=True)
        th_s[...] += dot_exact(pick, jnp.broadcast_to(through, (8, LANES)), (((0,), (1,)), ((), ())))

    def forward(s):
        def one(k, carry):
            j = s - n - k

            @pl.when(jnp.logical_and(j >= 0, j < n - 1))
            def _():
                for w in range(2):
                    hop(j, k, w, gat.at[j, k, w]).wait_recv()

                    @pl.when(j < n - 2)
                    def _():
                        hop(j + 1, k, w, gat.at[j, k, w]).start()

            return carry

        lax.fori_loop(0, pairs, one, 0)

    def arrange():
        for o in range(1, nh):
            hcopy(o).wait()

        def place(slot, src, q):
            tokmat[slot, q * quarter:(q + 1) * quarter, :] = tokall[
                lax.rem(h - q + nh, nh), lax.rem(d - src + n, n)].astype(bf16)

        def one(slot, carry):
            for q in range(nh):
                p = pos + n - slot if q < nh // 2 else pos + slot
                place(slot, member(lax.rem(p, n)), q)
            return carry

        lax.fori_loop(0, n, one, 0)

    def weights(k):
        blocks = [jnp.concatenate([pg_s[k + i, w] for i in range(2)], axis=1).astype(bf16)
                  for w in range(2)]
        for j in range(n - 1):
            for w in range(2):
                blocks.append(jnp.concatenate(
                    [gat[j, k + i, w] for i in range(2)], axis=1).astype(bf16))
        wg_ref[:, pl.ds(pl.multiple_of(k * LANES, 2 * LANES), 2 * LANES)] = dot_f32(
            tokmat[...].reshape(n * rows, tokmat.shape[2]), jnp.concatenate(blocks, axis=0), ROWS)

    def input_part(o):
        tcols = part.shape[1]
        to = lax.rem(h + o, nh)
        part[o] = dot_f32(xw[pl.ds(pl.multiple_of(to * tcols, tcols), tcols), :], pg_t[...])
        if o:
            gcopy(o).start()

    def chain(s, carry):
        if ring:
            forward(s)
        kf = s - d

        @pl.when(jnp.logical_and(kf >= 0, kf < pairs))
        def _():
            @pl.when(d > 0)
            def _():
                fcopy(kf).wait_recv()

            @pl.when(d < n - 1)
            def _():
                out_f[kf] = jnp.exp(ce_s[kf, rows - 1:rows, :]) * prior[kf] + loc_f[kf]
                fcopy(kf).start()

        kb = s - (n - 1 - d)

        @pl.when(jnp.logical_and(kb >= 0, kb < pairs))
        def _():
            @pl.when(d < n - 1)
            def _():
                bcopy(kb).wait_recv()

            @pl.when(d > 0)
            def _():
                out_b[kb] = jnp.exp(ce_s[kb, rows - 1:rows, :]) * adj[kb] + loc_b[kb]
                bcopy(kb).start()

        @pl.when(s < pairs)
        def _():
            mix(s)

        ks = s - (n - 1)

        @pl.when(jnp.logical_and(ks >= 0, ks < pairs))
        def _():
            finish(ks)

        if ring:
            @pl.when(s == n - 2)
            def _():
                for o in range(1, n):
                    tcopy(o).wait()
                for o in range(1, nh):
                    hcopy(o).start()

            for o in range(nh):
                @pl.when(s == n - 1 + pairs + (o - 1) % nh)
                def _():
                    input_part(o)

            @pl.when(s == max(2 * n - 2, n + pairs + nh))
            def _():
                arrange()
        return carry

    total_steps = n - 1 + pairs + (n - 1 if ring else 0)
    lax.fori_loop(0, total_steps, chain, 0)

    strict_ones = (row_ids > col_ids).astype(f32)
    dg_ref[...] = (dot_exact(q1_s[...], lower_ones, ROWS)
                   + dot_exact(q2_s[...], strict_ones, (((0,), (1,)), ((), ()))) + th_s[:, 0:1])

    @pl.when(d < n - 1)
    def _():
        def one(k, carry):
            fcopy(k).wait_send()
            return carry
        lax.fori_loop(0, pairs, one, 0)

    @pl.when(d > 0)
    def _():
        def one(k, carry):
            bcopy(k).wait_send()
            return carry
        lax.fori_loop(0, pairs, one, 0)

    if ring:
        def each(k, carry):
            weights(2 * k)
            return carry

        lax.fori_loop(0, pairs // 2, each, 0)
        total = part[0]
        for o in range(1, nh):
            gcopy(o).wait()
            total = total + got[o]
        tg_ref[...] = jnp.transpose(total).astype(bf16)

        def drain(k, carry):
            for w in range(2):
                hop(0, k, w, pg_s.at[k, w]).wait_send()

                def one(j, carry):
                    hop(j, k, w, gat.at[j - 1, k, w]).wait_send()
                    return carry

                lax.fori_loop(1, n - 1, one, 0)
            return carry

        lax.fori_loop(0, pairs, drain, 0)


def span_call(n, nh, ring, *args):
    tokens, x_weight, b_input, _, log_decay, _, cotangent = args[:7]
    rows, width = cotangent.shape
    depth = tokens.shape[1]
    heads, state = log_decay.shape[0], b_input.shape[1]
    pairs = width // LANES
    vm = pl.BlockSpec(memory_space=pltpu.VMEM)
    wide = pltpu.VMEM((pairs, rows, LANES), f32)
    states = pltpu.VMEM((pairs, state, LANES), f32)
    dma = pltpu.SemaphoreType.DMA
    scratch = [
        pltpu.VMEM((pairs, rows, LANES), bf16), wide, wide, wide, pltpu.VMEM((heads, rows), f32),
        wide, wide, pltpu.VMEM((rows, rows), f32), states, states, states, states, states, states,
        pltpu.VMEM((rows, heads), f32), pltpu.VMEM((rows, heads), f32), pltpu.VMEM((heads, 8), f32),
        pltpu.VMEM(x_weight.shape, bf16), dma(()), dma((pairs,)), dma((pairs,)), dma((pairs,)), dma((pairs,))]
    y = jax.ShapeDtypeStruct((rows, width), bf16)
    dg = jax.ShapeDtypeStruct((heads, rows), f32)
    if ring:
        cols, tcols = depth // n, depth // nh
        outs = [y, dg, jax.ShapeDtypeStruct((cols, width), f32), jax.ShapeDtypeStruct((rows, tcols), bf16)]
        out_part = pltpu.VMEM((nh, tcols, rows), f32)
        scratch += [
            pltpu.VMEM((pairs, 2, rows // 2, LANES), f32), pltpu.VMEM((width, rows), bf16),
            pltpu.VMEM((n - 1, pairs, 2, rows // 2, LANES), f32),
            pltpu.VMEM((n, rows // nh, cols), f32), pltpu.VMEM((nh, n, rows // nh, cols), f32), pltpu.VMEM((n, rows, cols), bf16), out_part, out_part,
            dma((n - 1, pairs, 2)), dma((n - 1, pairs, 2)), dma((n,)), dma((n,)),
            dma((nh,)), dma((nh,)), dma((nh,)), dma((nh,))]
    else:
        outs = [y, jax.ShapeDtypeStruct((rows, width), f32), dg]
    return pl.pallas_call(
        functools.partial(span_kernel, n, nh, ring),
        out_shape=outs,
        in_specs=[vm, pl.BlockSpec(memory_space=pl.ANY)] + [vm] * (len(args) - 2),
        out_specs=[vm] * len(outs),
        scratch_shapes=scratch,
        compiler_params=pltpu.CompilerParams(
            collective_id=0, has_side_effects=True, vmem_limit_bytes=60 << 20),
        cost_estimate=pl.CostEstimate(
            flops=6 * rows * depth * width, bytes_accessed=12 << 20, transcendentals=1 << 20),
        name="span",
    )(*args)


def hand_kernel(count, *refs):
    ins, outs, mids = refs[:count], refs[count:2 * count], refs[2 * count:3 * count]
    sems = refs[3 * count]
    first = [pltpu.make_async_copy(a, m, sems.at[0, i]) for i, (a, m) in enumerate(zip(ins, mids))]
    second = [pltpu.make_async_copy(m, b, sems.at[1, i]) for i, (m, b) in enumerate(zip(mids, outs))]
    for copy in first:
        copy.start()
    for one, two in zip(first, second):
        one.wait()
        two.start()
    for copy in second:
        copy.wait()


def hand_over(*arrays):
    anywhere = pl.BlockSpec(memory_space=pl.ANY)
    count = len(arrays)
    return pl.pallas_call(
        functools.partial(hand_kernel, count),
        out_shape=[jax.ShapeDtypeStruct(a.shape, a.dtype) for a in arrays],
        in_specs=[anywhere] * count,
        out_specs=[anywhere] * count,
        scratch_shapes=[pltpu.VMEM(a.shape, a.dtype) for a in arrays]
        + [pltpu.SemaphoreType.DMA((2, count))],
        name="hand_over",
    )(*arrays)


def per_device(tokens, x_weight, b_input, c_input, log_decay, step_size, cotangent):
    n, nh = lax.axis_size("seq"), lax.axis_size("head")
    rows, depth = tokens.shape
    assert rows == SPAN and n % 2 == 0
    ring = 4 <= n <= 8
    args = (tokens, x_weight, b_input, c_input, log_decay.T, step_size.T, cotangent)
    if ring:
        y, dg, wg, tg = span_call(n, nh, True, *args)
        y, wg, tg = hand_over(y, wg, tg)
        return y, tg, wg, dg.T
    y, pg, dg = span_call(n, nh, False, *args)
    pgb = pg.astype(bf16)
    wg = lax.psum_scatter(dot_f32(tokens, pgb, ROWS), "seq", scatter_dimension=0, tiled=True)
    tg = lax.psum_scatter(dot_f32(pgb, x_weight, COLS), "head", scatter_dimension=1, tiled=True)
    return y, tg.astype(bf16), wg, dg.T


def solution(mesh):
    return jax.shard_map(
        per_device,
        mesh=mesh,
        in_specs=(
            P("seq", None),
            P(None, "head"),
            P("seq", None),
            P("seq", None),
            P("seq", "head"),
            P("seq", "head"),
            P("seq", "head"),
        ),
        out_specs=(P("seq", "head"), P("seq", "head"), P("seq", "head"), P("seq", "head")),
        check_vma=False,
    )
```

```python
import functools

import jax
import jax.numpy as jnp
from jax import lax
from jax.experimental import pallas as pl
from jax.experimental.pallas import tpu as pltpu
from jax.sharding import PartitionSpec as P

SPAN = 256
LANES = 128
MESH = pl.DeviceIdType.MESH
highest = lax.Precision.HIGHEST
f32 = jnp.float32
bf16 = jnp.bfloat16


def dot_f32(a, b, dims=(((1,), (0,)), ((), ()))):
    return lax.dot_general(a, b, dims, preferred_element_type=f32)


def dot_exact(a, b, dims=(((1,), (0,)), ((), ()))):
    return lax.dot_general(a, b, dims, preferred_element_type=f32, precision=highest)


ROWS = (((0,), (0,)), ((), ()))
COLS = (((1,), (1,)), ((), ()))


def split_two(a):
    high = a.astype(bf16)
    return high, (a - high.astype(f32)).astype(bf16)


def span_kernel(n, nh, ring, *refs):
    tok, xw_hbm, b_ref, c_ref, ld, st, cot = refs[:7]
    refs = refs[7:]
    if ring:
        y_ref, dg_ref, wg_ref, tg_ref = refs[:4]
        refs = refs[4:]
    else:
        y_ref, pg_ref, dg_ref = refs[:3]
        refs = refs[3:]
    (x_s, pre_s, ce_s, st_s, cum_t, inner_s, back_s, score_s, loc_f, loc_b, out_f, out_b,
     prior, adj, q1_s, q2_s, th_s, xw, xw_sem, send_f, recv_f, send_b, recv_b) = refs[:23]
    if ring:
        (pg_s, pg_t, gat, tsend, tokall, tokmat, part, got, r_send, r_recv, t_send, t_recv, h_send, h_recv,
         g_send, g_recv) = refs[23:]
    d, h = lax.axis_index("seq"), lax.axis_index("head")
    rows, width = cot.shape
    heads = ld.shape[0]
    hdim = width // heads
    pairs = width // LANES
    per = LANES // hdim
    quarter, half = rows // nh, rows // 2
    load = pltpu.make_async_copy(xw_hbm, xw, xw_sem)
    load.start()

    barrier = pltpu.get_barrier_semaphore()
    for o in range(1, n) if ring else (1, n - 1):
        pl.semaphore_signal(barrier, 1, device_id={"seq": lax.rem(d + o, n)}, device_id_type=MESH)
    if ring:
        for o in range(1, nh):
            pl.semaphore_signal(barrier, 1, device_id={"head": lax.rem(h + o, nh)}, device_id_type=MESH)
    pl.semaphore_wait(barrier, n + nh - 2 if ring else 2)

    if ring:
        side = lax.rem(d, 2)
        pos = jnp.where(side == 0, d // 2, n - 1 - d // 2)

        def member(p):
            return jnp.where(p < n // 2, 2 * p, 2 * (n - 1 - p) + 1)

        next_to = (member(lax.rem(pos + 1, n)), member(lax.rem(pos + n - 1, n)))

        def tcopy(o):
            to = lax.rem(d + o, n)
            return pltpu.make_async_remote_copy(
                src_ref=tsend.at[to], dst_ref=tokall.at[0, o], send_sem=t_send.at[o],
                recv_sem=t_recv.at[o], device_id={"seq": to}, device_id_type=MESH)

        def hcopy(o):
            return pltpu.make_async_remote_copy(
                src_ref=tokall.at[0], dst_ref=tokall.at[o], send_sem=h_send.at[o],
                recv_sem=h_recv.at[o], device_id={"head": lax.rem(h + o, nh)}, device_id_type=MESH)

        def gcopy(o):
            return pltpu.make_async_remote_copy(
                src_ref=part.at[o], dst_ref=got.at[o], send_sem=g_send.at[o], recv_sem=g_recv.at[o],
                device_id={"head": lax.rem(h + o, nh)}, device_id_type=MESH)

        def hop(j, k, w, src):
            return pltpu.make_async_remote_copy(
                src_ref=src, dst_ref=gat.at[j, k, w], send_sem=r_send.at[j, k, w],
                recv_sem=r_recv.at[j, k, w], device_id={"seq": next_to[w]}, device_id_type=MESH)

        mine = tok[pl.ds(pl.multiple_of(h * quarter, quarter), quarter), :]
        tcols = tsend.shape[2]
        for i in range(n):
            tsend[i] = mine[:, i * tcols:(i + 1) * tcols].astype(f32)
        tokall[0, 0] = tsend[d]
        for o in range(1, n):
            tcopy(o).start()

    row_ids = lax.broadcasted_iota(jnp.int32, (rows, rows), 0)
    col_ids = lax.broadcasted_iota(jnp.int32, (rows, rows), 1)
    lower = row_ids >= col_ids
    lower_ones = lower.astype(f32)
    decay = ld[...]
    cum = dot_exact(lower_ones, decay, COLS)
    cum_t[...] = dot_exact(decay, lower_ones, COLS)
    spread = (lax.broadcasted_iota(jnp.int32, (heads, width), 0)
              == lax.broadcasted_iota(jnp.int32, (heads, width), 1) // hdim).astype(f32)
    wide_cum = dot_exact(cum, spread)
    wide_step = dot_exact(st[...], spread, ROWS)
    for p in range(pairs):
        ce_s[p] = wide_cum[:, p * LANES:(p + 1) * LANES]
        st_s[p] = wide_step[:, p * LANES:(p + 1) * LANES]
    b_val, c_val = b_ref[...], c_ref[...]
    score_s[...] = jnp.where(lower, dot_f32(c_val, b_val, COLS), 0.0)
    q1_s[...] = jnp.zeros_like(q1_s)
    q2_s[...] = jnp.zeros_like(q2_s)
    th_s[...] = jnp.zeros_like(th_s)

    load.wait()
    step_cols = 2 * LANES
    for k in range(width // step_cols):
        cols = slice(k * step_cols, (k + 1) * step_cols)
        ce = wide_cum[:, cols]
        gw = (cot[:, cols].astype(f32) * jnp.exp(ce)).astype(bf16)
        grad_k = dot_f32(c_val, gw, ROWS)
        pre = dot_f32(tok[...], xw[:, cols])
        act = pre / (1.0 + jnp.exp(-pre))
        xk = (act * wide_step[:, cols]).astype(bf16)
        xwk = (xk.astype(f32) * jnp.exp(ce[rows - 1:rows] - ce)).astype(bf16)
        state_k = dot_f32(b_val, xwk, ROWS)
        for i in range(2):
            at = slice(i * LANES, (i + 1) * LANES)
            pre_s[2 * k + i] = pre[:, at]
            x_s[2 * k + i] = xk[:, at]
            loc_b[2 * k + i] = grad_k[:, at]
            loc_f[2 * k + i] = state_k[:, at]

    @pl.when(d == 0)
    def _():
        prior[...] = jnp.zeros_like(prior)

    @pl.when(d == n - 1)
    def _():
        adj[...] = jnp.zeros_like(adj)

    def fcopy(k):
        return pltpu.make_async_remote_copy(
            src_ref=out_f.at[k], dst_ref=prior.at[k], send_sem=send_f.at[k], recv_sem=recv_f.at[k],
            device_id={"seq": lax.rem(d + 1, n)}, device_id_type=MESH)

    def bcopy(k):
        return pltpu.make_async_remote_copy(
            src_ref=out_b.at[k], dst_ref=adj.at[k], send_sem=send_b.at[k], recv_sem=recv_b.at[k],
            device_id={"seq": lax.rem(d + n - 1, n)}, device_id_type=MESH)

    lane = lax.broadcasted_iota(jnp.int32, (rows, LANES), 1)

    def mix(p):
        ce = ce_s[p]
        xp = x_s[p]
        gp = cot[:, pl.ds(pl.multiple_of(p * LANES, LANES), LANES)]
        inner = back = None
        for i in range(per):
            gap = ce[:, i * hdim:i * hdim + 1] - cum_t[pl.ds(per * p + i, 1), :]
            m = (score_s[...] * jnp.exp(jnp.minimum(gap, 0.0))).astype(bf16)
            inner_i = dot_f32(m, xp)
            back_i = dot_f32(m, gp, ROWS)
            if inner is None:
                inner, back = inner_i, back_i
            else:
                inner = jnp.where(lane < i * hdim, inner, inner_i)
                back = jnp.where(lane < i * hdim, back, back_i)
        inner_s[p] = inner
        back_s[p] = back

    def finish_grad(p):
        ce = ce_s[p]
        end = ce[rows - 1:rows]
        at = pl.ds(pl.multiple_of(p * LANES, LANES), LANES)
        hi, lo = split_two(adj[p])
        bc = jnp.exp(end - ce) * (dot_f32(b_val, hi) + dot_f32(b_val, lo))
        bi = back_s[p]
        pre = pre_s[p]
        sig = 1.0 / (1.0 + jnp.exp(-pre))
        pg = (bi + bc) * st_s[p] * sig * (1.0 + pre * (1.0 - sig))
        pg = pg.astype(bf16).astype(f32)
        if ring:
            pg_t[at, :] = jnp.transpose(pg).astype(bf16)
            pg_s[p, 0] = pg[:half]
            pg_s[p, 1] = pg[half:]
            for w in range(2):
                hop(0, p, w, pg_s.at[p, w]).start()
        else:
            pg_ref[:, at] = pg
        q2_s[...] += dot_exact(x_s[p].astype(f32) * bc, picker(p))

    def picker(p):
        return (lax.broadcasted_iota(jnp.int32, (LANES, heads), 0) // hdim + per * p
                == lax.broadcasted_iota(jnp.int32, (LANES, heads), 1)).astype(f32)

    def finish(p):
        ce = ce_s[p]
        end = ce[rows - 1:rows]
        at = pl.ds(pl.multiple_of(p * LANES, LANES), LANES)
        pr, ad = prior[p], adj[p]
        bi = back_s[p]
        grad = cot[:, at].astype(f32)
        x = x_s[p].astype(f32)
        hi, lo = split_two(pr)
        y = inner_s[p] + jnp.exp(ce) * (dot_f32(c_val, hi) + dot_f32(c_val, lo))
        y_ref[:, at] = y.astype(bf16)
        pick = picker(p)
        q1_s[...] += dot_exact(grad * y - x * bi, pick)
        through = jnp.exp(end) * jnp.sum(pr * ad, axis=0, keepdims=True)
        th_s[...] += dot_exact(pick, jnp.broadcast_to(through, (8, LANES)), (((0,), (1,)), ((), ())))

    def forward(s):
        def one(j, carry):
            sources = (member(lax.rem(pos + n - 1 - j, n)), member(lax.rem(pos + 1 + j, n)))
            for w in range(2):
                k = s - (n - sources[w] + j)

                @pl.when(jnp.logical_and(k >= 0, k < pairs))
                def _():
                    hop(j, k, w, gat.at[j, k, w]).wait_recv()

                    @pl.when(j < n - 2)
                    def _():
                        hop(j + 1, k, w, gat.at[j, k, w]).start()

            return carry

        lax.fori_loop(0, n - 1, one, 0)

    def arrange():
        for o in range(1, nh):
            hcopy(o).wait()

        def place(slot, src, q):
            tokmat[slot, q * quarter:(q + 1) * quarter, :] = tokall[
                lax.rem(h - q + nh, nh), lax.rem(d - src + n, n)].astype(bf16)

        def one(slot, carry):
            for q in range(nh):
                p = pos + n - slot if q < nh // 2 else pos + slot
                place(slot, member(lax.rem(p, n)), q)
            return carry

        lax.fori_loop(0, n, one, 0)

    def weights(k):
        blocks = [jnp.concatenate([pg_s[k + i, w] for i in range(2)], axis=1).astype(bf16)
                  for w in range(2)]
        for j in range(n - 1):
            for w in range(2):
                blocks.append(jnp.concatenate(
                    [gat[j, k + i, w] for i in range(2)], axis=1).astype(bf16))
        wg_ref[:, pl.ds(pl.multiple_of(k * LANES, 2 * LANES), 2 * LANES)] = dot_f32(
            tokmat[...].reshape(n * rows, tokmat.shape[2]), jnp.concatenate(blocks, axis=0), ROWS)

    def input_part(o):
        tcols = part.shape[1]
        to = lax.rem(h + o, nh)
        part[o] = dot_f32(xw[pl.ds(pl.multiple_of(to * tcols, tcols), tcols), :], pg_t[...])
        if o:
            gcopy(o).start()

    def chain(s, carry):
        if ring:
            forward(s)
        kf = s - d

        @pl.when(jnp.logical_and(kf >= 0, kf < pairs))
        def _():
            @pl.when(d > 0)
            def _():
                fcopy(kf).wait_recv()

            @pl.when(d < n - 1)
            def _():
                out_f[kf] = jnp.exp(ce_s[kf, rows - 1:rows, :]) * prior[kf] + loc_f[kf]
                fcopy(kf).start()

        kb = s - (n - 1 - d)

        @pl.when(jnp.logical_and(kb >= 0, kb < pairs))
        def _():
            @pl.when(d < n - 1)
            def _():
                bcopy(kb).wait_recv()

            @pl.when(d > 0)
            def _():
                out_b[kb] = jnp.exp(ce_s[kb, rows - 1:rows, :]) * adj[kb] + loc_b[kb]
                bcopy(kb).start()

        @pl.when(s < pairs)
        def _():
            mix(s)

        @pl.when(jnp.logical_and(kb >= 0, kb < pairs))
        def _():
            finish_grad(kb)

        ks = s - (n - 1)

        @pl.when(jnp.logical_and(ks >= 0, ks < pairs))
        def _():
            finish(ks)

        if ring:
            @pl.when(s == n - 2)
            def _():
                for o in range(1, n):
                    tcopy(o).wait()
                for o in range(1, nh):
                    hcopy(o).start()

            for o in range(nh):
                @pl.when(s == n - 1 - d + pairs + (o - 1) % nh)
                def _():
                    input_part(o)

            @pl.when(s == max(2 * n - 2, n + pairs + nh))
            def _():
                arrange()
        return carry

    total_steps = n - 1 + pairs + (n - 1 if ring else 0)
    lax.fori_loop(0, total_steps, chain, 0)

    strict_ones = (row_ids > col_ids).astype(f32)
    dg_ref[...] = (dot_exact(q1_s[...], lower_ones, ROWS)
                   + dot_exact(q2_s[...], strict_ones, (((0,), (1,)), ((), ()))) + th_s[:, 0:1])

    @pl.when(d < n - 1)
    def _():
        def one(k, carry):
            fcopy(k).wait_send()
            return carry
        lax.fori_loop(0, pairs, one, 0)

    @pl.when(d > 0)
    def _():
        def one(k, carry):
            bcopy(k).wait_send()
            return carry
        lax.fori_loop(0, pairs, one, 0)

    if ring:
        def each(k, carry):
            weights(2 * k)
            return carry

        lax.fori_loop(0, pairs // 2, each, 0)
        total = part[0]
        for o in range(1, nh):
            gcopy(o).wait()
            total = total + got[o]
        tg_ref[...] = jnp.transpose(total).astype(bf16)

        def drain(k, carry):
            for w in range(2):
                hop(0, k, w, pg_s.at[k, w]).wait_send()

                def one(j, carry):
                    hop(j, k, w, gat.at[j - 1, k, w]).wait_send()
                    return carry

                lax.fori_loop(1, n - 1, one, 0)
            return carry

        lax.fori_loop(0, pairs, drain, 0)


def span_call(n, nh, ring, *args):
    tokens, x_weight, b_input, _, log_decay, _, cotangent = args[:7]
    rows, width = cotangent.shape
    depth = tokens.shape[1]
    heads, state = log_decay.shape[0], b_input.shape[1]
    pairs = width // LANES
    vm = pl.BlockSpec(memory_space=pltpu.VMEM)
    wide = pltpu.VMEM((pairs, rows, LANES), f32)
    states = pltpu.VMEM((pairs, state, LANES), f32)
    dma = pltpu.SemaphoreType.DMA
    scratch = [
        pltpu.VMEM((pairs, rows, LANES), bf16), wide, wide, wide, pltpu.VMEM((heads, rows), f32),
        wide, wide, pltpu.VMEM((rows, rows), f32), states, states, states, states, states, states,
        pltpu.VMEM((rows, heads), f32), pltpu.VMEM((rows, heads), f32), pltpu.VMEM((heads, 8), f32),
        pltpu.VMEM(x_weight.shape, bf16), dma(()), dma((pairs,)), dma((pairs,)), dma((pairs,)), dma((pairs,))]
    y = jax.ShapeDtypeStruct((rows, width), bf16)
    dg = jax.ShapeDtypeStruct((heads, rows), f32)
    if ring:
        cols, tcols = depth // n, depth // nh
        outs = [y, dg, jax.ShapeDtypeStruct((cols, width), f32), jax.ShapeDtypeStruct((rows, tcols), bf16)]
        out_part = pltpu.VMEM((nh, tcols, rows), f32)
        scratch += [
            pltpu.VMEM((pairs, 2, rows // 2, LANES), f32), pltpu.VMEM((width, rows), bf16),
            pltpu.VMEM((n - 1, pairs, 2, rows // 2, LANES), f32),
            pltpu.VMEM((n, rows // nh, cols), f32), pltpu.VMEM((nh, n, rows // nh, cols), f32), pltpu.VMEM((n, rows, cols), bf16), out_part, out_part,
            dma((n - 1, pairs, 2)), dma((n - 1, pairs, 2)), dma((n,)), dma((n,)),
            dma((nh,)), dma((nh,)), dma((nh,)), dma((nh,))]
    else:
        outs = [y, jax.ShapeDtypeStruct((rows, width), f32), dg]
    return pl.pallas_call(
        functools.partial(span_kernel, n, nh, ring),
        out_shape=outs,
        in_specs=[vm, pl.BlockSpec(memory_space=pl.ANY)] + [vm] * (len(args) - 2),
        out_specs=[vm] * len(outs),
        scratch_shapes=scratch,
        compiler_params=pltpu.CompilerParams(
            collective_id=0, has_side_effects=True, vmem_limit_bytes=60 << 20),
        cost_estimate=pl.CostEstimate(
            flops=6 * rows * depth * width, bytes_accessed=12 << 20, transcendentals=1 << 20),
        name="span",
    )(*args)


def hand_kernel(count, *refs):
    ins, outs, mids = refs[:count], refs[count:2 * count], refs[2 * count:3 * count]
    sems = refs[3 * count]
    first = [pltpu.make_async_copy(a, m, sems.at[0, i]) for i, (a, m) in enumerate(zip(ins, mids))]
    second = [pltpu.make_async_copy(m, b, sems.at[1, i]) for i, (m, b) in enumerate(zip(mids, outs))]
    for copy in first:
        copy.start()
    for one, two in zip(first, second):
        one.wait()
        two.start()
    for copy in second:
        copy.wait()


def hand_over(*arrays):
    anywhere = pl.BlockSpec(memory_space=pl.ANY)
    count = len(arrays)
    return pl.pallas_call(
        functools.partial(hand_kernel, count),
        out_shape=[jax.ShapeDtypeStruct(a.shape, a.dtype) for a in arrays],
        in_specs=[anywhere] * count,
        out_specs=[anywhere] * count,
        scratch_shapes=[pltpu.VMEM(a.shape, a.dtype) for a in arrays]
        + [pltpu.SemaphoreType.DMA((2, count))],
        name="hand_over",
    )(*arrays)


def per_device(tokens, x_weight, b_input, c_input, log_decay, step_size, cotangent):
    n, nh = lax.axis_size("seq"), lax.axis_size("head")
    rows, depth = tokens.shape
    assert rows == SPAN and n % 2 == 0
    ring = 4 <= n <= 8
    args = (tokens, x_weight, b_input, c_input, log_decay.T, step_size.T, cotangent)
    if ring:
        y, dg, wg, tg = span_call(n, nh, True, *args)
        y, wg, tg = hand_over(y, wg, tg)
        return y, tg, wg, dg.T
    y, pg, dg = span_call(n, nh, False, *args)
    pgb = pg.astype(bf16)
    wg = lax.psum_scatter(dot_f32(tokens, pgb, ROWS), "seq", scatter_dimension=0, tiled=True)
    tg = lax.psum_scatter(dot_f32(pgb, x_weight, COLS), "head", scatter_dimension=1, tiled=True)
    return y, tg.astype(bf16), wg, dg.T


def solution(mesh):
    return jax.shard_map(
        per_device,
        mesh=mesh,
        in_specs=(
            P("seq", None),
            P(None, "head"),
            P("seq", None),
            P("seq", None),
            P("seq", "head"),
            P("seq", "head"),
            P("seq", "head"),
        ),
        out_specs=(P("seq", "head"), P("seq", "head"), P("seq", "head"), P("seq", "head")),
        check_vma=False,
    )
```
